32 devices in a mesh: rot: 8 (over y, x, core), az: 4 (over z).
Axes of the slice: x: 2, y: 2, z: 4, core: 2. Of those that a mesh axis runs over, the one named last changes fastest.
Arguments:
- inputs: bfloat16 [16, 4, 128, 128], P('rot', None, 'az'), may hold values from -6 to 6
- pre_one: bfloat16 [16, 4, 128, 128], P('rot', None, 'az'), may hold values from -8 to 8
- pre_two: bfloat16 [16, 4, 128, 128], P('rot', None, 'az'), may hold values from -8 to 8
- cotangent: bfloat16 [16, 4, 128, 128], P('rot', None, 'az'), may hold values from -6 to 6
- filt_one: bfloat16 [16, 3, 3, 128, 128], P('rot'), may hold values from -0.046875 to 0.046875
- filt_two: bfloat16 [16, 3, 3, 128, 128], P('rot'), may hold values from -0.046875 to 0.046875
Outputs:
- input_grad: bfloat16 [16, 4, 128, 128], P('rot', None, 'az')
- filt_grad_one: float32 [16, 3, 3, 128, 128], P('rot')
- filt_grad_two: float32 [16, 3, 3, 128, 128], P('rot')
The draws below stay inside these ranges and needn't reach their ends.
All inputs are finite; a program needn't handle non-finite values.
Results may differ from the reference program's by a relative error of at most 0.018.
Values may be sent and summed in bfloat16 or wider, within the bound.
A program may use at most 64 MiB of HBM per device.

```python
import jax
import jax.numpy as jnp
from jax import lax

R = 16
C = 128
H = 4
AZ = 128


def block_scale(own_key, extent, shards, smallest, top_value):
    def one(dim, blocks):
        heights = jax.random.uniform(jax.random.fold_in(jax.random.fold_in(own_key, 6), dim), (blocks,), jnp.float32, smallest / len(shards), top_value / len(shards))
        return jnp.repeat(jnp.exp(heights), extent[dim] // blocks).reshape((-1,) + (1,) * (len(extent) - dim - 1))

    level = one(*shards[0])
    for cut in shards[1:]:
        level = level * one(*cut)
    return level


def gaussian(key, extent, scale, reach, cuts=(), kind=jnp.bfloat16):
    drawn = jax.random.normal(key, extent, jnp.float32) * scale
    if len(cuts) > 0:
        drawn = block_scale(key, extent, cuts, -0.22, 0.18) * drawn
    return jnp.clip(drawn, min=-reach, max=reach).astype(kind)


def setup_inputs(seed: int = 0) -> dict:
    key_of = jax.random.split(jax.random.key(seed), 7)
    inputs = gaussian(key_of[0], (R, H, AZ, C), 1.0, 6.0, ((0, 8), (2, 4)))
    pre_one = gaussian(key_of[1], (R, H, AZ, C), 1.5, 8.0, ((0, 8), (2, 4)))
    pre_two = gaussian(key_of[2], (R, H, AZ, C), 1.5, 8.0, ((0, 8), (2, 4)))
    cotangent = gaussian(key_of[3], (R, H, AZ, C), 1.0, 6.0, ((0, 8), (2, 4)))
    filt_one = gaussian(key_of[4], (R, 3, 3, C, C), (9 * R * C) ** -0.5, 0.046875, ((0, 8),))
    filt_two = gaussian(key_of[5], (R, 3, 3, C, C), (9 * R * C) ** -0.5, 0.046875, ((0, 8),))
    return dict(inputs=inputs, pre_one=pre_one, pre_two=pre_two, cotangent=cotangent, filt_one=filt_one, filt_two=filt_two)


def wrap_pad(field):
    widened = jnp.concatenate([field[:, :, -1:], field, field[:, :, :1]], axis=2)
    return jnp.pad(widened, ((0, 0), (1, 1), (0, 0), (0, 0)))

def slope(pre):
    widened = pre.astype(jnp.float32)
    logistic = jax.nn.sigmoid(widened)
    return logistic * (1.0 + widened * (1.0 - logistic))

def data_grad(gradient, filters):
    padded = wrap_pad(gradient.astype(jnp.float32))
    weights = filters.astype(jnp.float32)
    orient = jnp.arange(R, dtype=jnp.int32)

    def single(target):
        chosen = padded[(target - orient) % R]
        summed = jnp.zeros((H, AZ, C), jnp.float32)
        for row_tap in range(3):
            for col_tap in range(3):
                window = chosen[:, 2 - row_tap:2 - row_tap + H, 2 - col_tap:2 - col_tap + AZ, :]
                summed = summed + jnp.einsum('ryxc,ric->yxi', window, weights[:, row_tap, col_tap], precision=lax.Precision.HIGHEST)
        return summed
    return lax.map(single, orient)

def weight_grad(features, gradient):
    padded = wrap_pad(features.astype(jnp.float32))
    widened = gradient.astype(jnp.float32)
    orient = jnp.arange(R, dtype=jnp.int32)

    def single(relative):
        shifted = padded[(orient + relative) % R]
        pieces = []
        for row_tap in range(3):
            for col_tap in range(3):
                window = shifted[:, row_tap:row_tap + H, col_tap:col_tap + AZ, :]
                pieces.append(jnp.einsum('gyxi,gyxo->io', window, widened, precision=lax.Precision.HIGHEST))
        return jnp.stack(pieces).reshape(3, 3, C, C)
    return lax.map(single, orient)

def reference(inputs, pre_one, pre_two, cotangent, filt_one, filt_two):
    scale = (R * H * AZ) ** (-0.5)
    act_one = jax.nn.silu(pre_one.astype(jnp.float32)).astype(jnp.bfloat16)
    grad_two = (cotangent.astype(jnp.float32) * slope(pre_two)).astype(jnp.bfloat16)
    filt_grad_two = weight_grad(act_one, grad_two) * scale
    delta_one = data_grad(grad_two, filt_two)
    grad_one = (delta_one * slope(pre_one)).astype(jnp.bfloat16)
    input_grad = data_grad(grad_one, filt_one).astype(jnp.bfloat16)
    filt_grad_one = weight_grad(inputs, grad_one) * scale
    return (input_grad, filt_grad_one, filt_grad_two)
```

```python
import functools

import jax
import jax.numpy as jnp
from jax import lax
from jax.experimental import pallas as pl
from jax.experimental.pallas import tpu as pltpu
from jax.sharding import PartitionSpec as P

F32 = jnp.float32
BF16 = jnp.bfloat16


def slope(v):
    s = jax.nn.sigmoid(v)
    return s * (1.0 + v * (1.0 - s))


def kernel(
    n, m, p, H, X, C, scale,
    inputs, pre_one, pre_two, cot, filt_one, filt_two,
    out_in, out_f1, out_f2,
    st_g, st_e, st_a, grads, edges, feats, weights, gx, lhs, outs,
    part_s, part_r, zs, zr, zt, za,
    g_ss, g_rs, e_ss, e_rs, a_ss, a_rs, p_ss, p_rs, z_ss, z_rs, y_ss, y_rs,
):
    R = n * p
    HX = H * X
    me = lax.axis_index("rot")
    z = lax.axis_index("az")

    def rank(q):
        return lax.rem(me + q, n)

    def col(d):
        return lax.rem(z + d, m)

    def copy(src, dst, ss, rs, rot, az):
        return pltpu.make_async_remote_copy(
            src_ref=src, dst_ref=dst, send_sem=ss, recv_sem=rs,
            device_id={"rot": rot, "az": az}, device_id_type=pl.DeviceIdType.MESH,
        )

    barrier = pltpu.get_barrier_semaphore()
    near = sorted({0, 1 % m, (m - 1) % m})
    partners = [(q, d) for d in near for q in range(n)]
    partners += [(0, d) for d in range(m) if d not in near]
    partners = [pair for pair in partners if pair != (0, 0)]
    for q, d in partners:
        pl.semaphore_signal(
            barrier, inc=1, device_id={"rot": rank(q), "az": col(d)},
            device_id_type=pl.DeviceIdType.MESH,
        )

    pending = []

    def start(c):
        c.start()
        pending.append(c)
        return c

    def stage_grad(ph, value):
        st_g[ph] = value.astype(BF16)
        grads[ph, me] = value.astype(BF16)
        st_e[ph, 0] = value[:, :, 0, :].reshape(p * H, C)
        st_e[ph, 1] = value[:, :, X - 1, :].reshape(p * H, C)

    def send_grad(ph):
        g_copies = [
            start(copy(st_g.at[ph], grads.at[ph, me], g_ss.at[ph, q], g_rs.at[ph, q], rank(q), z))
            for q in range(1, n)
        ]
        for q in range(n):
            for side, d in ((1, 1), (0, m - 1)):
                g_copies.append(
                    start(
                        copy(
                            st_e.at[ph, side], edges.at[ph, 1 - side, me],
                            e_ss.at[ph, side, q], e_rs.at[ph, side, q], rank(q), col(d),
                        )
                    )
                )
        return g_copies

    def stage_feat(ph, value):
        for o in range(p):
            turned = value[o].T.astype(BF16)
            st_a[ph, o] = turned
            feats[ph, 0, o] = turned

    def send_feat(ph):
        return [
            start(copy(st_a.at[ph], feats.at[ph, n - q], a_ss.at[ph, q], a_rs.at[ph, q], rank(q), z))
            for q in range(1, n)
        ]

    def build_gx(ph):
        x_of = lax.broadcasted_iota(jnp.int32, (p * H, X, C), 1).reshape(p * HX, C)

        def body(d, carry):
            g = grads[ph, d].astype(F32).reshape(p * HX, C)
            low = jnp.broadcast_to(edges[ph, 0, d][:, None, :], (p * H, X, C)).reshape(p * HX, C)
            high = jnp.broadcast_to(edges[ph, 1, d][:, None, :], (p * H, X, C)).reshape(p * HX, C)
            before = jnp.where(x_of == 0, low, pltpu.roll(g, 1, 0))
            after = jnp.where(x_of == X - 1, high, pltpu.roll(g, p * HX - 1, 0))
            for j, v in enumerate((after, g, before)):
                gx[pl.ds(d * p, p), 1 : H + 1, :, j * C : (j + 1) * C] = v.astype(BF16).reshape(p, H, X, C)
            return carry

        lax.fori_loop(0, n, body, 0)

    def build_weights(filt):
        for s in range(p):
            for i in range(3):
                for j in range(3):
                    weights[s * C : (s + 1) * C, (i * 3 + j) * C : (i * 3 + j + 1) * C] = filt[s, i, j]

    def build_lhs(ph):
        lane = lax.broadcasted_iota(jnp.int32, (C, HX), 1)
        for q in range(n):
            for o in range(p):
                block = q * p + o
                a = feats[ph, q, o]
                wide = a.astype(F32)
                down = jnp.where(lane < X, 0.0, pltpu.roll(wide, X, 1)).astype(BF16)
                up = jnp.where(lane >= HX - X, 0.0, pltpu.roll(wide, HX - X, 1)).astype(BF16)
                spots = [block] + ([R + block] if block < p - 1 else [])
                for spot in spots:
                    for i, v in enumerate((down, a, up)):
                        lhs[i * C : (i + 1) * C, spot * HX : (spot + 1) * HX] = v

    def data_terms(ph):
        copies = []
        w = weights[...]

        def product(q):
            rows = jnp.concatenate(
                [gx[q * p : (q + 1) * p, 2 - i : 2 - i + H].reshape(p * HX, 3 * C) for i in range(3)],
                axis=1,
            )
            got = lax.dot_general(rows, w, (((1,), (1,)), ((), ())), preferred_element_type=F32)
            outs[q * p : (q + 1) * p] = got.reshape(p, HX, p * C)

        def emit(q):
            for o in range(p):
                total = None
                for s in range(p):
                    term = outs[(q * p + o - s) % R, :, s * C : (s + 1) * C]
                    total = term if total is None else total + term
                if q == 0:
                    part_r[ph, 0, o] = total.astype(BF16)
                else:
                    part_s[ph, q, o] = total.astype(BF16)
            if q > 0:
                copies.append(
                    start(
                        copy(part_s.at[ph, q], part_r.at[ph, q], p_ss.at[ph, q], p_rs.at[ph, q], rank(q), z)
                    )
                )

        for q in range(n):
            product(q)
            if q > 0:
                emit(q)
        emit(0)
        return copies

    def part_sum(ph, copies):
        for c in copies:
            c.wait_recv()
        total = part_r[ph, 0].astype(F32)
        for q in range(1, n):
            total = total + part_r[ph, q].astype(F32)
        return total

    K = p * 9
    cm = C // m

    def filt_terms(ph):
        right = gx[:, 1 : H + 1].reshape(R * HX, 3 * C)
        for s in range(p):
            got = jnp.dot(
                lhs[:, s * HX : (s + R) * HX], right, preferred_element_type=F32
            )
            for i in range(3):
                for j in range(3):
                    tile = got[i * C : (i + 1) * C, j * C : (j + 1) * C].astype(F32).reshape(m, cm, C)
                    zs[ph, :, s * 9 + i * 3 + j] = tile.astype(BF16)
        return [
            start(copy(zs.at[ph, col(d)], zr.at[ph, d], z_ss.at[ph, d], z_rs.at[ph, d], me, col(d)))
            for d in range(1, m)
        ]

    def filt_sum(ph, copies):
        for c in copies:
            c.wait_recv()
        total = zs[ph, z].astype(F32)
        for d in range(1, m):
            total = total + zr[ph, d].astype(F32)
        total = total.astype(BF16)
        zt[ph] = total
        za[ph, z] = total
        return [
            start(copy(zt.at[ph], za.at[ph, z], y_ss.at[ph, d], y_rs.at[ph, d], me, col(d)))
            for d in range(1, m)
        ]

    def filt_out(ph, copies, out):
        for c in copies:
            c.wait_recv()
        for c in range(m):
            out[:, :, :, c * cm : (c + 1) * cm, :] = (za[ph, c].astype(F32) * scale).reshape(p, 3, 3, cm, C)

    grad_two = (cot[...].astype(F32) * slope(pre_two[...].astype(F32))).astype(BF16).astype(F32)
    stage_grad(0, grad_two)
    wide_one = pre_one[...].astype(F32)
    stage_feat(0, (wide_one * jax.nn.sigmoid(wide_one)).reshape(p, HX, C))
    stage_feat(1, inputs[...].astype(F32).reshape(p, HX, C))
    pl.semaphore_wait(barrier, len(partners))

    g_copies = send_grad(0)
    a_copies = send_feat(0)
    i_copies = send_feat(1)
    build_weights(filt_two)
    gx[:, 0] = jnp.zeros((R, X, 3 * C), BF16)
    gx[:, H + 1] = jnp.zeros((R, X, 3 * C), BF16)
    for c in g_copies:
        c.wait_recv()
    build_gx(0)
    p_copies = data_terms(0)
    for c in a_copies:
        c.wait_recv()
    build_lhs(0)
    z_copies = filt_terms(0)

    delta = part_sum(0, p_copies).reshape(p, H, X, C)
    grad_one = (delta * slope(pre_one[...].astype(F32))).astype(BF16).astype(F32)
    stage_grad(1, grad_one)
    g_copies = send_grad(1)
    build_weights(filt_one)
    for c in i_copies:
        c.wait_recv()
    build_lhs(1)
    for c in g_copies:
        c.wait_recv()
    build_gx(1)
    p_copies = data_terms(1)
    w_copies = filt_terms(1)
    y_two = filt_sum(0, z_copies)
    out_in[...] = part_sum(1, p_copies).astype(BF16).reshape(p, H, X, C)
    y_one = filt_sum(1, w_copies)
    filt_out(0, y_two, out_f2)
    filt_out(1, y_one, out_f1)
    for c in pending:
        c.wait_send()


def solution(mesh):
    n, m = mesh.shape["rot"], mesh.shape["az"]

    def shards(inputs, pre_one, pre_two, cot, filt_one, filt_two):
        p, H, X, C = inputs.shape
        R, HX, K, cm = n * p, H * X, p * 9, C // m
        scale = float(R * H * X * m) ** -0.5
        dma = pltpu.SemaphoreType.DMA
        vmem = pl.BlockSpec(memory_space=pltpu.VMEM)
        filt = jax.ShapeDtypeStruct((p, 3, 3, C, C), F32)
        return pl.pallas_call(
            functools.partial(kernel, n, m, p, H, X, C, scale),
            out_shape=(jax.ShapeDtypeStruct((p, H, X, C), BF16), filt, filt),
            in_specs=[vmem] * 6,
            out_specs=(vmem,) * 3,
            scratch_shapes=[
                pltpu.VMEM((2, p, H, X, C), BF16),
                pltpu.VMEM((2, 2, p * H, C), F32),
                pltpu.VMEM((2, p, C, HX), BF16),
                pltpu.VMEM((2, n, p, H, X, C), BF16),
                pltpu.VMEM((2, 2, n, p * H, C), F32),
                pltpu.VMEM((2, n, p, C, HX), BF16),
                pltpu.VMEM((p * C, 9 * C), BF16),
                pltpu.VMEM((R, H + 2, X, 3 * C), BF16),
                pltpu.VMEM((3 * C, (R + p - 1) * HX), BF16),
                pltpu.VMEM((R, HX, p * C), F32),
                pltpu.VMEM((2, n, p, HX, C), BF16),
                pltpu.VMEM((2, n, p, HX, C), BF16),
                pltpu.VMEM((2, m, K, cm, C), BF16),
                pltpu.VMEM((2, m, K, cm, C), BF16),
                pltpu.VMEM((2, K, cm, C), BF16),
                pltpu.VMEM((2, m, K, cm, C), BF16),
                dma((2, n)), dma((2, n)),
                dma((2, 2, n)), dma((2, 2, n)),
                dma((2, n)), dma((2, n)),
                dma((2, n)), dma((2, n)),
                dma((2, m)), dma((2, m)),
                dma((2, m)), dma((2, m)),
            ],
            compiler_params=pltpu.CompilerParams(
                collective_id=0, has_side_effects=True, vmem_limit_bytes=60 * 1024 * 1024
            ),
        )(inputs, pre_one, pre_two, cot, filt_one, filt_two)

    cells = P("rot", None, "az", None)
    banks = P("rot", None, None, None, None)
    return jax.shard_map(
        shards, mesh=mesh,
        in_specs=(cells,) * 4 + (banks,) * 2,
        out_specs=(cells, banks, banks),
        check_vma=False,
    )
```

```python
import functools

import jax
import jax.numpy as jnp
from jax import lax
from jax.experimental import pallas as pl
from jax.experimental.pallas import tpu as pltpu
from jax.sharding import PartitionSpec as P

F32 = jnp.float32
BF16 = jnp.bfloat16


def slope(v):
    s = jax.nn.sigmoid(v)
    return s * (1.0 + v * (1.0 - s))


def kernel(
    n, m, p, H, X, C,
    inputs, pre_one, pre_two, cot, filt_one, filt_two,
    out_in, out_f1, out_f2,
    st_g, st_e, st_a, grads, edges, feats, weights, gx, lhs, outs,
    part_s, part_x, part_m, part_r, zs, zr, zt,
    g_ss, g_rs, gf_ss, gf_rs, e_ss, e_rs, ef_ss, ef_rs, a_ss, a_rs, af_ss, af_rs,
    x_ss, x_rs, p_ss, p_rs, z_ss, z_rs, y_ss, y_rs,
):
    R = n * p
    HX = H * X
    nc = n // 2
    half = C // 2
    K = 3 * p
    me = lax.axis_index("rot")
    z = lax.axis_index("az")
    core = lax.rem(me, 2)
    chip = lax.div(me, 2)
    sib = me + 1 - 2 * core

    def to(t):
        return 2 * lax.rem(chip + t, nc) + core

    def frm(t):
        return 2 * lax.rem(chip + nc - t, nc) + core

    def col(d):
        return lax.rem(z + d, m)

    def copy(src, dst, ss, rs, rot, az):
        return pltpu.make_async_remote_copy(
            src_ref=src, dst_ref=dst, send_sem=ss, recv_sem=rs,
            device_id={"rot": rot, "az": az}, device_id_type=pl.DeviceIdType.MESH,
        )

    barrier = pltpu.get_barrier_semaphore()
    near_cols = sorted({1 % m, (m - 1) % m})
    partners = [(sib, z)] + [(to(t), z) for t in range(1, nc)]
    partners += [(to(t), col(d)) for d in near_cols for t in range(nc)]
    for rot, az in partners:
        pl.semaphore_signal(
            barrier, inc=1, device_id={"rot": rot, "az": az},
            device_id_type=pl.DeviceIdType.MESH,
        )

    pending = []

    def start(c):
        c.start()
        pending.append(c)
        return c

    def stage_grad(ph, value):
        st_g[ph] = value.astype(BF16)
        grads[ph, me] = value.astype(BF16)
        st_e[ph, 0] = value[:, :, 0, :].reshape(p * H, C).astype(BF16)
        st_e[ph, 1] = value[:, :, X - 1, :].reshape(p * H, C).astype(BF16)

    def send_grad(ph):
        direct = [None] + [
            start(copy(st_g.at[ph], grads.at[ph, me], g_ss.at[ph, t], g_rs.at[ph, t], to(t), z))
            for t in range(1, nc)
        ]
        own = start(copy(st_g.at[ph], grads.at[ph, me], gf_ss.at[ph, 0], gf_rs.at[ph, 0], sib, z))
        rims = []
        for t in range(nc):
            for side, d in ((1, 1), (0, m - 1)):
                rims.append(
                    start(
                        copy(
                            st_e.at[ph, side], edges.at[ph, me, 1 - side],
                            e_ss.at[ph, side, t], e_rs.at[ph, side, t], to(t), col(d),
                        )
                    )
                )
        return direct, own, rims

    def relay_grad(ph, sent):
        direct, own, rims = sent
        passed = [own]
        for t in range(nc):
            rims[2 * t].wait_recv()
            rims[2 * t + 1].wait_recv()
            d = frm(t)
            passed.append(
                start(copy(edges.at[ph, d], edges.at[ph, d], ef_ss.at[ph, t], ef_rs.at[ph, t], sib, z))
            )
        for t in range(1, nc):
            direct[t].wait_recv()
            d = frm(t)
            passed.append(
                start(copy(grads.at[ph, d], grads.at[ph, d], gf_ss.at[ph, t], gf_rs.at[ph, t], sib, z))
            )
        return passed

    def stage_feat(ph, value):
        for o in range(p):
            turned = value[o].T.astype(BF16)
            st_a[ph, o] = turned
            feats[ph, me, o] = turned

    def send_feat(ph):
        direct = [None] + [
            start(copy(st_a.at[ph], feats.at[ph, me], a_ss.at[ph, t], a_rs.at[ph, t], to(t), z))
            for t in range(1, nc)
        ]
        own = start(copy(st_a.at[ph], feats.at[ph, me], af_ss.at[ph, 0], af_rs.at[ph, 0], sib, z))
        return direct, own

    def relay_feat(ph, sent):
        direct, own = sent
        passed = [own]
        for t in range(1, nc):
            direct[t].wait_recv()
            d = frm(t)
            passed.append(
                start(copy(feats.at[ph, d], feats.at[ph, d], af_ss.at[ph, t], af_rs.at[ph, t], sib, z))
            )
        return passed

    def arrive(copies):
        for c in copies:
            c.wait_recv()

    def build_gx(ph):
        x_of = lax.broadcasted_iota(jnp.int32, (p * H, X, C), 1).reshape(p * HX, C)

        def body(d, carry):
            g = grads[ph, d].astype(F32).reshape(p * HX, C)
            low = edges[ph, d, 0].astype(F32)
            high = edges[ph, d, 1].astype(F32)
            low = jnp.broadcast_to(low[:, None, :], (p * H, X, C)).reshape(p * HX, C)
            high = jnp.broadcast_to(high[:, None, :], (p * H, X, C)).reshape(p * HX, C)
            before = jnp.where(x_of == 0, low, pltpu.roll(g, 1, 0))
            after = jnp.where(x_of == X - 1, high, pltpu.roll(g, p * HX - 1, 0))
            for j, v in enumerate((after, g, before)):
                gx[pl.ds(d * p, p), 1 : H + 1, :, j * C : (j + 1) * C] = v.astype(BF16).reshape(p, H, X, C)
            return carry

        lax.fori_loop(0, n, body, 0)

    def build_weights(filt):
        for s in range(p):
            for i in range(3):
                for j in range(3):
                    weights[s * C : (s + 1) * C, (i * 3 + j) * C : (i * 3 + j + 1) * C] = filt[s, i, j]

    def build_lhs(ph):
        lane = lax.broadcasted_iota(jnp.int32, (C, HX), 1)
        for q in range(n):
            owner = lax.rem(me + q, n)
            for o in range(p):
                block = q * p + o
                a = feats[ph, owner, o]
                wide = a.astype(F32)
                down = jnp.where(lane < X, 0.0, pltpu.roll(wide, X, 1)).astype(BF16)
                up = jnp.where(lane >= HX - X, 0.0, pltpu.roll(wide, HX - X, 1)).astype(BF16)
                spots = [block] + ([R + block] if block < p - 1 else [])
                for spot in spots:
                    for i, v in enumerate((down, a, up)):
                        lhs[i * C : (i + 1) * C, spot * HX : (spot + 1) * HX] = v

    def term(q, o):
        total = None
        for s in range(p):
            one = outs[(q * p + o - s) % R, :, s * C : (s + 1) * C]
            total = one if total is None else total + one
        return total

    def data_terms(ph):
        w = weights[...]
        crossed = [None] * n

        def emit(q):
            for o in range(p):
                part_s[ph, q, o] = term(q, o).astype(BF16)
            t = lax.rem(q // 2 + core, nc)
            crossed[q] = start(
                copy(part_s.at[ph, q], part_x.at[ph, t], x_ss.at[ph, t], x_rs.at[ph, t], sib, z)
            )

        for q in range(n):
            rows = jnp.concatenate(
                [gx[q * p : (q + 1) * p, 2 - i : 2 - i + H].reshape(p * HX, 3 * C) for i in range(3)],
                axis=1,
            )
            got = lax.dot_general(rows, w, (((1,), (1,)), ((), ())), preferred_element_type=F32)
            outs[q * p : (q + 1) * p] = got.reshape(p, HX, p * C)
            if q % 2 == 1:
                emit(q)

    def merge_terms(ph):
        sent = []
        for t in list(range(1, nc)) + [0]:
            pltpu.make_async_remote_copy(
                src_ref=part_x.at[ph, t], dst_ref=part_x.at[ph, t],
                send_sem=x_ss.at[ph, t], recv_sem=x_rs.at[ph, t],
                device_id={"rot": sib, "az": z}, device_id_type=pl.DeviceIdType.MESH,
            ).wait_recv()
            for o in range(p):
                total = term(2 * t, o) + part_x[ph, t, o].astype(F32)
                if t == 0:
                    part_r[ph, 0, o] = total.astype(BF16)
                else:
                    part_m[ph, t, o] = total.astype(BF16)
            if t > 0:
                sent.append(
                    start(
                        copy(part_m.at[ph, t], part_r.at[ph, t], p_ss.at[ph, t], p_rs.at[ph, t], to(t), z)
                    )
                )
        return sent

    def part_sum(ph, copies):
        arrive(copies)
        total = part_r[ph, 0].astype(F32)
        for t in range(1, nc):
            total = total + part_r[ph, t].astype(F32)
        return total

    fg = (out_f2, out_f1)
    lower = z < m // 2
    near_pos = jnp.where(lower, z, m - 1 - z)
    near_h = jnp.where(lower, 0, 1)
    far_h = 1 - near_h
    right, left = jnp.minimum(z + 1, m - 1), jnp.maximum(z - 1, 0)
    inner = jnp.where(lower, right, left)
    outer = jnp.where(lower, left, right)
    at_end = near_pos == 0

    def final(ph, h, k):
        return fg[ph].at[k, :, pl.ds(pl.multiple_of(h * half, half), half), :]

    def hop(src, ph, h, k, az):
        return copy(src, zr.at[ph, h, k], z_ss.at[ph, h, k], z_rs.at[ph, h, k], me, az)

    def back(ph, h, k, az):
        return copy(final(ph, h, k), final(ph, h, k), y_ss.at[ph, h, k], y_rs.at[ph, h, k], me, az)

    def filt_terms(ph):
        right_side = gx[:, 1 : H + 1].reshape(R * HX, 3 * C)
        for s in range(p):
            got = jnp.dot(
                lhs[:, s * HX : (s + R) * HX], right_side, preferred_element_type=F32
            )
            for i in range(3):
                k = s * 3 + i
                for j in range(3):
                    tile = got[i * C : (i + 1) * C, j * C : (j + 1) * C]
                    zs[ph, :, k, j] = tile.reshape(2, half, C).astype(BF16)

                @pl.when(at_end)
                def _():
                    hop(zs.at[ph, near_h, k], ph, near_h, k, inner).start()

    def near_sums(ph):
        @pl.when(jnp.logical_not(at_end))
        def _():
            for k in range(K):
                hop(zs.at[ph, near_h, k], ph, near_h, k, inner).wait_recv()
                zt[ph, near_h, k] = (
                    zs[ph, near_h, k].astype(F32) + zr[ph, near_h, k].astype(F32)
                ).astype(BF16)
                hop(zt.at[ph, near_h, k], ph, near_h, k, inner).start()

    def far_sums(ph):
        for k in range(K):
            hop(zs.at[ph, far_h, k], ph, far_h, k, outer).wait_recv()
            total = (zs[ph, far_h, k].astype(F32) + zr[ph, far_h, k].astype(F32)).astype(BF16)

            @pl.when(at_end)
            def _():
                fg[ph][k, :, pl.ds(pl.multiple_of(far_h * half, half), half), :] = total
                back(ph, far_h, k, inner).start()

            @pl.when(jnp.logical_not(at_end))
            def _():
                zt[ph, far_h, k] = total
                hop(zt.at[ph, far_h, k], ph, far_h, k, outer).start()

    def far_back(ph):
        @pl.when(jnp.logical_not(at_end))
        def _():
            for k in range(K):
                back(ph, far_h, k, inner).wait_recv()
                back(ph, far_h, k, inner).start()

    def near_back(ph):
        for k in range(K):
            back(ph, near_h, k, outer).wait_recv()

            @pl.when(jnp.logical_not(at_end))
            def _():
                back(ph, near_h, k, outer).start()

    def drain(ph):
        for k in range(K):
            hop(zs.at[ph, near_h, k], ph, near_h, k, inner).wait_send()
            back(ph, far_h, k, inner).wait_send()

        @pl.when(jnp.logical_not(at_end))
        def _():
            for k in range(K):
                hop(zt.at[ph, far_h, k], ph, far_h, k, outer).wait_send()
                back(ph, near_h, k, outer).wait_send()

    grad_two = (cot[...].astype(F32) * slope(pre_two[...].astype(F32))).astype(BF16).astype(F32)
    stage_grad(0, grad_two)
    pl.semaphore_wait(barrier, len(partners))
    g_sent = send_grad(0)
    wide_one = pre_one[...].astype(F32)
    stage_feat(0, (wide_one * jax.nn.sigmoid(wide_one)).reshape(p, HX, C))
    a_sent = send_feat(0)
    stage_feat(1, inputs[...].astype(F32).reshape(p, HX, C))
    build_weights(filt_two)
    gx[:, 0] = jnp.zeros((R, X, 3 * C), BF16)
    gx[:, H + 1] = jnp.zeros((R, X, 3 * C), BF16)
    arrive(relay_grad(0, g_sent))
    build_gx(0)
    data_terms(0)
    a_passed = relay_feat(0, a_sent)
    p_sent = merge_terms(0)
    i_sent = send_feat(1)
    arrive(a_passed)
    build_lhs(0)
    filt_terms(0)

    delta = part_sum(0, p_sent).reshape(p, H, X, C)
    grad_one = (delta * slope(pre_one[...].astype(F32))).astype(BF16).astype(F32)
    stage_grad(1, grad_one)
    g_sent = send_grad(1)
    build_weights(filt_one)
    i_passed = relay_feat(1, i_sent)
    near_sums(0)
    arrive(i_passed)
    build_lhs(1)
    g_passed = relay_grad(1, g_sent)
    far_sums(0)
    arrive(g_passed)
    build_gx(1)
    filt_terms(1)
    far_back(0)
    near_sums(1)
    data_terms(1)
    near_back(0)
    p_sent = merge_terms(1)
    far_sums(1)
    far_back(1)
    out_in[...] = part_sum(1, p_sent).astype(BF16).reshape(p, H, X, C)
    near_back(1)
    for c in pending:
        c.wait_send()
    drain(0)
    drain(1)


def solution(mesh):
    n, m = mesh.shape["rot"], mesh.shape["az"]

    def shards(inputs, pre_one, pre_two, cot, filt_one, filt_two):
        p, H, X, C = inputs.shape
        R, HX, K, nc = n * p, H * X, 3 * p, n // 2
        scale = float(R * H * X * m) ** -0.5
        dma = pltpu.SemaphoreType.DMA
        vmem = pl.BlockSpec(memory_space=pltpu.VMEM)
        sums = jax.ShapeDtypeStruct((K, 3, C, C), BF16)
        got, sum_one, sum_two = pl.pallas_call(
            functools.partial(kernel, n, m, p, H, X, C),
            out_shape=(jax.ShapeDtypeStruct((p, H, X, C), BF16), sums, sums),
            in_specs=[vmem] * 6,
            out_specs=(vmem,) * 3,
            scratch_shapes=[
                pltpu.VMEM((2, p, H, X, C), BF16),
                pltpu.VMEM((2, 2, p * H, C), BF16),
                pltpu.VMEM((2, p, C, HX), BF16),
                pltpu.VMEM((2, n, p, H, X, C), BF16),
                pltpu.VMEM((2, n, 2, p * H, C), BF16),
                pltpu.VMEM((2, n, p, C, HX), BF16),
                pltpu.VMEM((p * C, 9 * C), BF16),
                pltpu.VMEM((R, H + 2, X, 3 * C), BF16),
                pltpu.VMEM((3 * C, (R + p - 1) * HX), BF16),
                pltpu.VMEM((R, HX, p * C), F32),
                pltpu.VMEM((2, n, p, HX, C), BF16),
                pltpu.VMEM((2, nc, p, HX, C), BF16),
                pltpu.VMEM((2, nc, p, HX, C), BF16),
                pltpu.VMEM((2, nc, p, HX, C), BF16),
                pltpu.VMEM((2, 2, K, 3, C // 2, C), BF16),
                pltpu.VMEM((2, 2, K, 3, C // 2, C), BF16),
                pltpu.VMEM((2, 2, K, 3, C // 2, C), BF16),
            ]
            + [dma((2, nc))] * 4
            + [dma((2, 2, nc))] * 2
            + [dma((2, nc))] * 2
            + [dma((2, nc))] * 8
            + [dma((2, 2, K))] * 4,
            compiler_params=pltpu.CompilerParams(
                collective_id=0, has_side_effects=True, vmem_limit_bytes=60 * 1024 * 1024
            ),
        )(inputs, pre_one, pre_two, cot, filt_one, filt_two)

        def widen(v):
            return (v.astype(F32) * scale).reshape(p, 3, 3, C, C)

        return got, widen(sum_one), widen(sum_two)

    cells = P("rot", None, "az", None)
    banks = P("rot", None, None, None, None)
    return jax.shard_map(
        shards, mesh=mesh,
        in_specs=(cells,) * 4 + (banks,) * 2,
        out_specs=(cells, banks, banks),
        check_vma=False,
    )
```

```python
import functools

import jax
import jax.numpy as jnp
from jax import lax
from jax.experimental import pallas as pl
from jax.experimental.pallas import tpu as pltpu
from jax.sharding import PartitionSpec as P

F32 = jnp.float32
BF16 = jnp.bfloat16


def slope(v):
    s = jax.nn.sigmoid(v)
    return s * (1.0 + v * (1.0 - s))


def kernel(
    n, m, p, H, X, C,
    inputs, pre_one, pre_two, cot, filt_one, filt_two,
    out_in, out_f1, out_f2,
    st_g, st_e, st_a, grads, edges, feats, weights, gx, lhs, outs,
    part_s, part_x, part_m, part_r, zs, zr, zt,
    g_ss, g_rs, gf_ss, gf_rs, e_ss, e_rs, ef_ss, ef_rs, a_ss, a_rs, af_ss, af_rs,
    x_ss, x_rs, p_ss, p_rs, z_ss, z_rs, y_ss, y_rs,
):
    R = n * p
    HX = H * X
    nc = n // 2
    K = 9 * p
    me = lax.axis_index("rot")
    z = lax.axis_index("az")
    core = lax.rem(me, 2)
    chip = lax.div(me, 2)
    sib = me + 1 - 2 * core

    def to(t):
        return 2 * lax.rem(chip + t, nc) + core

    def frm(t):
        return 2 * lax.rem(chip + nc - t, nc) + core

    def col(d):
        return lax.rem(z + d, m)

    def copy(src, dst, ss, rs, rot, az):
        return pltpu.make_async_remote_copy(
            src_ref=src, dst_ref=dst, send_sem=ss, recv_sem=rs,
            device_id={"rot": rot, "az": az}, device_id_type=pl.DeviceIdType.MESH,
        )

    barrier = pltpu.get_barrier_semaphore()
    near_cols = sorted({1 % m, (m - 1) % m})
    partners = [(sib, z)] + [(to(t), z) for t in range(1, nc)]
    partners += [(to(t), col(d)) for d in near_cols for t in range(nc)]
    for rot, az in partners:
        pl.semaphore_signal(
            barrier, inc=1, device_id={"rot": rot, "az": az},
            device_id_type=pl.DeviceIdType.MESH,
        )

    pending = []

    def start(c):
        c.start()
        pending.append(c)
        return c

    def stage_grad(ph, value):
        st_g[ph] = value.astype(BF16)
        grads[ph, me] = value.astype(BF16)
        st_e[ph, 0] = value[:, :, 0, :].reshape(p * H, C).astype(BF16)
        st_e[ph, 1] = value[:, :, X - 1, :].reshape(p * H, C).astype(BF16)

    def send_grad(ph):
        direct = [None] + [
            start(copy(st_g.at[ph], grads.at[ph, me], g_ss.at[ph, t], g_rs.at[ph, t], to(t), z))
            for t in range(1, nc)
        ]
        own = start(copy(st_g.at[ph], grads.at[ph, me], gf_ss.at[ph, 0], gf_rs.at[ph, 0], sib, z))
        rims = []
        for t in range(nc):
            for side, d in ((1, 1), (0, m - 1)):
                rims.append(
                    start(
                        copy(
                            st_e.at[ph, side], edges.at[ph, me, 1 - side],
                            e_ss.at[ph, side, t], e_rs.at[ph, side, t], to(t), col(d),
                        )
                    )
                )
        return direct, own, rims

    def relay_grad(ph, sent):
        direct, own, rims = sent
        passed = [own]
        for t in range(nc):
            rims[2 * t].wait_recv()
            rims[2 * t + 1].wait_recv()
            d = frm(t)
            passed.append(
                start(copy(edges.at[ph, d], edges.at[ph, d], ef_ss.at[ph, t], ef_rs.at[ph, t], sib, z))
            )
        for t in range(1, nc):
            direct[t].wait_recv()
            d = frm(t)
            passed.append(
                start(copy(grads.at[ph, d], grads.at[ph, d], gf_ss.at[ph, t], gf_rs.at[ph, t], sib, z))
            )
        return passed

    def stage_feat(ph, value):
        for o in range(p):
            turned = value[o].T.astype(BF16)
            st_a[ph, o] = turned
            feats[ph, me, o] = turned

    def send_feat(ph):
        direct = [None] + [
            start(copy(st_a.at[ph], feats.at[ph, me], a_ss.at[ph, t], a_rs.at[ph, t], to(t), z))
            for t in range(1, nc)
        ]
        own = start(copy(st_a.at[ph], feats.at[ph, me], af_ss.at[ph, 0], af_rs.at[ph, 0], sib, z))
        return direct, own

    def relay_feat(ph, sent):
        direct, own = sent
        passed = [own]
        for t in range(1, nc):
            direct[t].wait_recv()
            d = frm(t)
            passed.append(
                start(copy(feats.at[ph, d], feats.at[ph, d], af_ss.at[ph, t], af_rs.at[ph, t], sib, z))
            )
        return passed

    def arrive(copies):
        for c in copies:
            c.wait_recv()

    def build_gx(ph):
        x_of = lax.broadcasted_iota(jnp.int32, (p * H, X, C), 1).reshape(p * HX, C)

        def body(d, carry):
            g = grads[ph, d].astype(F32).reshape(p * HX, C)
            low = edges[ph, d, 0].astype(F32)
            high = edges[ph, d, 1].astype(F32)
            low = jnp.broadcast_to(low[:, None, :], (p * H, X, C)).reshape(p * HX, C)
            high = jnp.broadcast_to(high[:, None, :], (p * H, X, C)).reshape(p * HX, C)
            before = jnp.where(x_of == 0, low, pltpu.roll(g, 1, 0))
            after = jnp.where(x_of == X - 1, high, pltpu.roll(g, p * HX - 1, 0))
            for j, v in enumerate((after, g, before)):
                gx[pl.ds(d * p, p), 1 : H + 1, :, j * C : (j + 1) * C] = v.astype(BF16).reshape(p, H, X, C)
            return carry

        lax.fori_loop(0, n, body, 0)

    def build_weights(filt):
        for s in range(p):
            for i in range(3):
                for j in range(3):
                    weights[s * C : (s + 1) * C, (i * 3 + j) * C : (i * 3 + j + 1) * C] = filt[s, i, j]

    def build_lhs(ph):
        lane = lax.broadcasted_iota(jnp.int32, (C, HX), 1)
        for q in range(n):
            owner = lax.rem(me + q, n)
            for o in range(p):
                block = q * p + o
                a = feats[ph, owner, o]
                wide = a.astype(F32)
                down = jnp.where(lane < X, 0.0, pltpu.roll(wide, X, 1)).astype(BF16)
                up = jnp.where(lane >= HX - X, 0.0, pltpu.roll(wide, HX - X, 1)).astype(BF16)
                spots = [block] + ([R + block] if block < p - 1 else [])
                for spot in spots:
                    for i, v in enumerate((down, a, up)):
                        lhs[i * C : (i + 1) * C, spot * HX : (spot + 1) * HX] = v

    def term(q, o):
        total = None
        for s in range(p):
            one = outs[(q * p + o - s) % R, :, s * C : (s + 1) * C]
            total = one if total is None else total + one
        return total

    def data_terms(ph):
        w = weights[...]
        crossed = [None] * n

        def emit(q):
            for o in range(p):
                part_s[ph, q, o] = term(q, o).astype(BF16)
            t = lax.rem(q // 2 + core, nc)
            crossed[q] = start(
                copy(part_s.at[ph, q], part_x.at[ph, t], x_ss.at[ph, t], x_rs.at[ph, t], sib, z)
            )

        for q in range(n):
            rows = jnp.concatenate(
                [gx[q * p : (q + 1) * p, 2 - i : 2 - i + H].reshape(p * HX, 3 * C) for i in range(3)],
                axis=1,
            )
            got = lax.dot_general(rows, w, (((1,), (1,)), ((), ())), preferred_element_type=F32)
            outs[q * p : (q + 1) * p] = got.reshape(p, HX, p * C)
            if q % 2 == 1:
                emit(q)

    def merge_terms(ph):
        sent = []
        for t in list(range(1, nc)) + [0]:
            pltpu.make_async_remote_copy(
                src_ref=part_x.at[ph, t], dst_ref=part_x.at[ph, t],
                send_sem=x_ss.at[ph, t], recv_sem=x_rs.at[ph, t],
                device_id={"rot": sib, "az": z}, device_id_type=pl.DeviceIdType.MESH,
            ).wait_recv()
            for o in range(p):
                total = term(2 * t, o) + part_x[ph, t, o].astype(F32)
                if t == 0:
                    part_r[ph, 0, o] = total.astype(BF16)
                else:
                    part_m[ph, t, o] = total.astype(BF16)
            if t > 0:
                sent.append(
                    start(
                        copy(part_m.at[ph, t], part_r.at[ph, t], p_ss.at[ph, t], p_rs.at[ph, t], to(t), z)
                    )
                )
        return sent

    def part_sum(ph, copies):
        arrive(copies)
        total = part_r[ph, 0].astype(F32)
        for t in range(1, nc):
            total = total + part_r[ph, t].astype(F32)
        return total

    fg = (out_f2, out_f1)
    lower = z < m // 2
    near_pos = jnp.where(lower, z, m - 1 - z)
    right, left = jnp.minimum(z + 1, m - 1), jnp.maximum(z - 1, 0)
    inner = jnp.where(lower, right, left)
    outer = jnp.where(lower, left, right)
    at_end = near_pos == 0
    at_mid = near_pos == m // 2 - 1
    slot = jnp.where(at_mid, 1, 0)

    def inward(src, ph, k):
        return copy(src, zr.at[ph, slot, k], z_ss.at[ph, k], z_rs.at[ph, slot, k], me, inner)

    def crossed_in(ph, w, k):
        return copy(zr.at[ph, w, k], zr.at[ph, w, k], z_ss.at[ph, k], z_rs.at[ph, w, k], me, inner)

    def outward(ph, k):
        return copy(fg[ph].at[k], fg[ph].at[k], y_ss.at[ph, k], y_rs.at[ph, k], me, outer)

    def filt_terms(ph):
        right_side = gx[:, 1 : H + 1].reshape(R * HX, 3 * C)
        for s in range(p):
            got = jnp.dot(
                lhs[:, s * HX : (s + R) * HX], right_side, preferred_element_type=F32
            )
            for i in range(3):
                for j in range(3):
                    zs[ph, (s * 3 + i) * 3 + j] = got[i * C : (i + 1) * C, j * C : (j + 1) * C].astype(BF16)

            @pl.when(at_end)
            def _():
                for k in range(s * 9, s * 9 + 9):
                    inward(zs.at[ph, k], ph, k).start()

    def go_in(ph, a, b):
        @pl.when(jnp.logical_not(at_end))
        def _():
            for k in range(K * a // 18, K * b // 18):
                crossed_in(ph, 0, k).wait_recv()
                zt[ph, k] = (zs[ph, k].astype(F32) + zr[ph, 0, k].astype(F32)).astype(BF16)
                inward(zt.at[ph, k], ph, k).start()

    base = zs if m == 2 else zt

    def go_out(ph, a, b):
        for k in range(K * a // 18, K * b // 18):

            @pl.when(at_mid)
            def _():
                crossed_in(ph, 1, k).wait_recv()
                fg[ph][k] = (base[ph, k].astype(F32) + zr[ph, 1, k].astype(F32)).astype(BF16)

            @pl.when(jnp.logical_not(at_mid))
            def _():
                outward(ph, k).wait_recv()

            @pl.when(jnp.logical_not(at_end))
            def _():
                outward(ph, k).start()

    def drain(ph):
        for k in range(K):
            crossed_in(ph, 0, k).wait_send()

        @pl.when(jnp.logical_not(at_end))
        def _():
            for k in range(K):
                outward(ph, k).wait_send()

    grad_two = (cot[...].astype(F32) * slope(pre_two[...].astype(F32))).astype(BF16).astype(F32)
    stage_grad(0, grad_two)
    pl.semaphore_wait(barrier, len(partners))
    g_sent = send_grad(0)
    wide_one = pre_one[...].astype(F32)
    stage_feat(0, (wide_one * jax.nn.sigmoid(wide_one)).reshape(p, HX, C))
    a_sent = send_feat(0)
    stage_feat(1, inputs[...].astype(F32).reshape(p, HX, C))
    build_weights(filt_two)
    gx[:, 0] = jnp.zeros((R, X, 3 * C), BF16)
    gx[:, H + 1] = jnp.zeros((R, X, 3 * C), BF16)
    arrive(relay_grad(0, g_sent))
    build_gx(0)
    data_terms(0)
    a_passed = relay_feat(0, a_sent)
    p_sent = merge_terms(0)
    i_sent = send_feat(1)
    arrive(a_passed)
    build_lhs(0)
    filt_terms(0)

    delta = part_sum(0, p_sent).reshape(p, H, X, C)
    grad_one = (delta * slope(pre_one[...].astype(F32))).astype(BF16).astype(F32)
    stage_grad(1, grad_one)
    g_sent = send_grad(1)
    i_passed = relay_feat(1, i_sent)
    go_in(0, 0, 2)
    build_weights(filt_one)
    arrive(i_passed)
    build_lhs(1)
    go_in(0, 2, 6)
    g_passed = relay_grad(1, g_sent)
    go_in(0, 6, 9)
    go_out(0, 0, 3)
    arrive(g_passed)
    build_gx(1)
    go_in(0, 9, 12)
    go_out(0, 3, 7)
    filt_terms(1)
    go_in(0, 12, 16)
    go_out(0, 7, 12)
    data_terms(1)
    go_in(0, 16, 18)
    p_sent = merge_terms(1)
    go_out(0, 12, 18)
    go_in(1, 0, 4)
    out_in[...] = part_sum(1, p_sent).astype(BF16).reshape(p, H, X, C)
    for k in range(4, 18):
        go_in(1, k, k + 1)
        go_out(1, k - 4, k - 3)
    go_out(1, 14, 18)
    for c in pending:
        c.wait_send()
    drain(0)
    drain(1)


def solution(mesh):
    n, m = mesh.shape["rot"], mesh.shape["az"]

    def shards(inputs, pre_one, pre_two, cot, filt_one, filt_two):
        p, H, X, C = inputs.shape
        R, HX, K, nc = n * p, H * X, 9 * p, n // 2
        scale = float(R * H * X * m) ** -0.5
        dma = pltpu.SemaphoreType.DMA
        vmem = pl.BlockSpec(memory_space=pltpu.VMEM)
        sums = jax.ShapeDtypeStruct((K, C, C), BF16)
        got, sum_one, sum_two = pl.pallas_call(
            functools.partial(kernel, n, m, p, H, X, C),
            out_shape=(jax.ShapeDtypeStruct((p, H, X, C), BF16), sums, sums),
            in_specs=[vmem] * 6,
            out_specs=(vmem,) * 3,
            scratch_shapes=[
                pltpu.VMEM((2, p, H, X, C), BF16),
                pltpu.VMEM((2, 2, p * H, C), BF16),
                pltpu.VMEM((2, p, C, HX), BF16),
                pltpu.VMEM((2, n, p, H, X, C), BF16),
                pltpu.VMEM((2, n, 2, p * H, C), BF16),
                pltpu.VMEM((2, n, p, C, HX), BF16),
                pltpu.VMEM((p * C, 9 * C), BF16),
                pltpu.VMEM((R, H + 2, X, 3 * C), BF16),
                pltpu.VMEM((3 * C, (R + p - 1) * HX), BF16),
                pltpu.VMEM((R, HX, p * C), F32),
                pltpu.VMEM((2, n, p, HX, C), BF16),
                pltpu.VMEM((2, nc, p, HX, C), BF16),
                pltpu.VMEM((2, nc, p, HX, C), BF16),
                pltpu.VMEM((2, nc, p, HX, C), BF16),
                pltpu.VMEM((2, K, C, C), BF16),
                pltpu.VMEM((2, 2, K, C, C), BF16),
                pltpu.VMEM((2, K, C, C), BF16),
            ]
            + [dma((2, nc))] * 4
            + [dma((2, 2, nc))] * 2
            + [dma((2, nc))] * 2
            + [dma((2, nc))] * 8
            + [dma((2, K)), dma((2, 2, K)), dma((2, K)), dma((2, K))],
            compiler_params=pltpu.CompilerParams(
                collective_id=0, has_side_effects=True, vmem_limit_bytes=60 * 1024 * 1024
            ),
        )(inputs, pre_one, pre_two, cot, filt_one, filt_two)

        def widen(v):
            return (v.astype(F32) * scale).reshape(p, 3, 3, C, C)

        return got, widen(sum_one), widen(sum_two)

    cells = P("rot", None, "az", None)
    banks = P("rot", None, None, None, None)
    return jax.shard_map(
        shards, mesh=mesh,
        in_specs=(cells,) * 4 + (banks,) * 2,
        out_specs=(cells, banks, banks),
        check_vma=False,
    )
```

```python
import functools

import jax
import jax.numpy as jnp
from jax import lax
from jax.experimental import pallas as pl
from jax.experimental.pallas import tpu as pltpu
from jax.sharding import PartitionSpec as P

F32 = jnp.float32
BF16 = jnp.bfloat16


def slope(v):
    s = jax.nn.sigmoid(v)
    return s * (1.0 + v * (1.0 - s))


def kernel(
    n, m, p, H, X, C,
    inputs, pre_one, pre_two, cot, filt_one, filt_two,
    out_in, out_f1, out_f2,
    st_g, st_e, st_a, grads, edges, feats, weights, gx, lhs, outs,
    part_s, part_x, part_m, part_r, zs, zr, zt,
    g_ss, g_rs, gf_ss, gf_rs, e_ss, e_rs, ef_ss, ef_rs, a_ss, a_rs, af_ss, af_rs,
    x_ss, x_rs, p_ss, p_rs, z_ss, z_rs, y_ss, y_rs,
):
    R = n * p
    HX = H * X
    nc = n // 2
    K = 9 * p
    me = lax.axis_index("rot")
    z = lax.axis_index("az")
    core = lax.rem(me, 2)
    chip = lax.div(me, 2)
    sib = me + 1 - 2 * core

    def to(t):
        return 2 * lax.rem(chip + t, nc) + core

    def frm(t):
        return 2 * lax.rem(chip + nc - t, nc) + core

    def col(d):
        return lax.rem(z + d, m)

    def copy(src, dst, ss, rs, rot, az):
        return pltpu.make_async_remote_copy(
            src_ref=src, dst_ref=dst, send_sem=ss, recv_sem=rs,
            device_id={"rot": rot, "az": az}, device_id_type=pl.DeviceIdType.MESH,
        )

    barrier = pltpu.get_barrier_semaphore()
    near_cols = sorted({1 % m, (m - 1) % m})
    partners = [(sib, z)] + [(to(t), z) for t in range(1, nc)]
    partners += [(to(t), col(d)) for d in near_cols for t in range(nc)]
    for rot, az in partners:
        pl.semaphore_signal(
            barrier, inc=1, device_id={"rot": rot, "az": az},
            device_id_type=pl.DeviceIdType.MESH,
        )

    pending = []

    def start(c):
        c.start()
        pending.append(c)
        return c

    def stage_grad(ph, value):
        st_g[ph] = value.astype(BF16)
        grads[ph, me] = value.astype(BF16)
        st_e[ph, 0] = value[:, :, 0, :].reshape(p * H, C).astype(BF16)
        st_e[ph, 1] = value[:, :, X - 1, :].reshape(p * H, C).astype(BF16)

    def send_grad(ph):
        direct = [None] + [
            start(copy(st_g.at[ph], grads.at[ph, me], g_ss.at[ph, t], g_rs.at[ph, t], to(t), z))
            for t in range(1, nc)
        ]
        own = start(copy(st_g.at[ph], grads.at[ph, me], gf_ss.at[ph, 0], gf_rs.at[ph, 0], sib, z))
        rims = []
        for t in range(nc):
            for side, d in ((1, 1), (0, m - 1)):
                rims.append(
                    start(
                        copy(
                            st_e.at[ph, side], edges.at[ph, me, 1 - side],
                            e_ss.at[ph, side, t], e_rs.at[ph, side, t], to(t), col(d),
                        )
                    )
                )
        return direct, own, rims

    def relay_grad(ph, sent):
        direct, own, rims = sent
        passed = [own]
        for t in range(nc):
            rims[2 * t].wait_recv()
            rims[2 * t + 1].wait_recv()
            d = frm(t)
            passed.append(
                start(copy(edges.at[ph, d], edges.at[ph, d], ef_ss.at[ph, t], ef_rs.at[ph, t], sib, z))
            )
        for t in range(1, nc):
            direct[t].wait_recv()
            d = frm(t)
            passed.append(
                start(copy(grads.at[ph, d], grads.at[ph, d], gf_ss.at[ph, t], gf_rs.at[ph, t], sib, z))
            )
        return passed

    def stage_feat(ph, value):
        for o in range(p):
            turned = value[o].T.astype(BF16)
            st_a[ph, o] = turned
            feats[ph, me, o] = turned

    def send_feat(ph):
        direct = [None] + [
            start(copy(st_a.at[ph], feats.at[ph, me], a_ss.at[ph, t], a_rs.at[ph, t], to(t), z))
            for t in range(1, nc)
        ]
        own = start(copy(st_a.at[ph], feats.at[ph, me], af_ss.at[ph, 0], af_rs.at[ph, 0], sib, z))
        return direct, own

    def relay_feat(ph, sent):
        direct, own = sent
        passed = [own]
        for t in range(1, nc):
            direct[t].wait_recv()
            d = frm(t)
            passed.append(
                start(copy(feats.at[ph, d], feats.at[ph, d], af_ss.at[ph, t], af_rs.at[ph, t], sib, z))
            )
        return passed

    def arrive(copies):
        for c in copies:
            c.wait_recv()

    def build_gx(ph):
        x_of = lax.broadcasted_iota(jnp.int32, (p * H, X, C), 1).reshape(p * HX, C)

        def body(d, carry):
            g = grads[ph, d].astype(F32).reshape(p * HX, C)
            low = edges[ph, d, 0].astype(F32)
            high = edges[ph, d, 1].astype(F32)
            low = jnp.broadcast_to(low[:, None, :], (p * H, X, C)).reshape(p * HX, C)
            high = jnp.broadcast_to(high[:, None, :], (p * H, X, C)).reshape(p * HX, C)
            before = jnp.where(x_of == 0, low, pltpu.roll(g, 1, 0))
            after = jnp.where(x_of == X - 1, high, pltpu.roll(g, p * HX - 1, 0))
            for j, v in enumerate((after, g, before)):
                gx[pl.ds(d * p, p), 1 : H + 1, :, j * C : (j + 1) * C] = v.astype(BF16).reshape(p, H, X, C)
            return carry

        lax.fori_loop(0, n, body, 0)

    def build_weights(filt):
        for s in range(p):
            for i in range(3):
                for j in range(3):
                    weights[s * C : (s + 1) * C, (i * 3 + j) * C : (i * 3 + j + 1) * C] = filt[s, i, j]

    def build_lhs(ph):
        lane = lax.broadcasted_iota(jnp.int32, (C, HX), 1)
        for q in range(n):
            owner = lax.rem(me + q, n)
            for o in range(p):
                block = q * p + o
                a = feats[ph, owner, o]
                wide = a.astype(F32)
                down = jnp.where(lane < X, 0.0, pltpu.roll(wide, X, 1)).astype(BF16)
                up = jnp.where(lane >= HX - X, 0.0, pltpu.roll(wide, HX - X, 1)).astype(BF16)
                spots = [block] + ([R + block] if block < p - 1 else [])
                for spot in spots:
                    for i, v in enumerate((down, a, up)):
                        lhs[i * C : (i + 1) * C, spot * HX : (spot + 1) * HX] = v

    def term(q, o):
        total = None
        for s in range(p):
            one = outs[(q * p + o - s) % R, :, s * C : (s + 1) * C]
            total = one if total is None else total + one
        return total

    def data_terms(ph):
        w = weights[...]
        crossed = [None] * n

        def emit(q):
            for o in range(p):
                part_s[ph, q, o] = term(q, o).astype(BF16)
            t = lax.rem(q // 2 + core, nc)
            crossed[q] = start(
                copy(part_s.at[ph, q], part_x.at[ph, t], x_ss.at[ph, t], x_rs.at[ph, t], sib, z)
            )

        for q in range(n):
            rows = jnp.concatenate(
                [gx[q * p : (q + 1) * p, 2 - i : 2 - i + H].reshape(p * HX, 3 * C) for i in range(3)],
                axis=1,
            )
            got = lax.dot_general(rows, w, (((1,), (1,)), ((), ())), preferred_element_type=F32)
            outs[q * p : (q + 1) * p] = got.reshape(p, HX, p * C)
            if q % 2 == 1:
                emit(q)

    def merge_terms(ph):
        sent = []
        for t in list(range(1, nc)) + [0]:
            pltpu.make_async_remote_copy(
                src_ref=part_x.at[ph, t], dst_ref=part_x.at[ph, t],
                send_sem=x_ss.at[ph, t], recv_sem=x_rs.at[ph, t],
                device_id={"rot": sib, "az": z}, device_id_type=pl.DeviceIdType.MESH,
            ).wait_recv()
            for o in range(p):
                total = term(2 * t, o) + part_x[ph, t, o].astype(F32)
                if t == 0:
                    part_r[ph, 0, o] = total.astype(BF16)
                else:
                    part_m[ph, t, o] = total.astype(BF16)
            if t > 0:
                sent.append(
                    start(
                        copy(part_m.at[ph, t], part_r.at[ph, t], p_ss.at[ph, t], p_rs.at[ph, t], to(t), z)
                    )
                )
        return sent

    def part_sum(ph, copies):
        arrive(copies)
        total = part_r[ph, 0].astype(F32)
        for t in range(1, nc):
            total = total + part_r[ph, t].astype(F32)
        return total

    fg = (out_f2, out_f1)
    lower = z < m // 2
    near_pos = jnp.where(lower, z, m - 1 - z)
    right, left = jnp.minimum(z + 1, m - 1), jnp.maximum(z - 1, 0)
    inner = jnp.where(lower, right, left)
    outer = jnp.where(lower, left, right)
    at_end = near_pos == 0
    at_mid = near_pos == m // 2 - 1
    slot = jnp.where(at_mid, 1, 0)

    def inward(src, ph, k):
        return copy(src, zr.at[ph, slot, k], z_ss.at[ph, k], z_rs.at[ph, slot, k], me, inner)

    def crossed_in(ph, w, k):
        return copy(zr.at[ph, w, k], zr.at[ph, w, k], z_ss.at[ph, k], z_rs.at[ph, w, k], me, inner)

    def outward(ph, k):
        return copy(fg[ph].at[k], fg[ph].at[k], y_ss.at[ph, k], y_rs.at[ph, k], me, outer)

    def filt_terms(ph):
        right_side = gx[:, 1 : H + 1].reshape(R * HX, 3 * C)
        for s in range(p):
            got = jnp.dot(
                lhs[:, s * HX : (s + R) * HX], right_side, preferred_element_type=F32
            )
            for i in range(3):
                for j in range(3):
                    zs[ph, (s * 3 + i) * 3 + j] = got[i * C : (i + 1) * C, j * C : (j + 1) * C].astype(BF16)

            if ph == 1:
                begin(ph, s * 18 // p, (s + 1) * 18 // p)

    def begin(ph, a, b):
        @pl.when(at_end)
        def _():
            for k in range(K * a // 18, K * b // 18):
                inward(zs.at[ph, k], ph, k).start()

    def go_in(ph, a, b):
        @pl.when(jnp.logical_not(at_end))
        def _():
            for k in range(K * a // 18, K * b // 18):
                crossed_in(ph, 0, k).wait_recv()
                zt[ph, k] = (zs[ph, k].astype(F32) + zr[ph, 0, k].astype(F32)).astype(BF16)
                inward(zt.at[ph, k], ph, k).start()

    base = zs if m == 2 else zt

    def go_out(ph, a, b):
        for k in range(K * a // 18, K * b // 18):

            @pl.when(at_mid)
            def _():
                crossed_in(ph, 1, k).wait_recv()
                fg[ph][k] = (base[ph, k].astype(F32) + zr[ph, 1, k].astype(F32)).astype(BF16)

            @pl.when(jnp.logical_not(at_mid))
            def _():
                outward(ph, k).wait_recv()

            @pl.when(jnp.logical_not(at_end))
            def _():
                outward(ph, k).start()

    def drain(ph):
        for k in range(K):
            crossed_in(ph, 0, k).wait_send()

        @pl.when(jnp.logical_not(at_end))
        def _():
            for k in range(K):
                outward(ph, k).wait_send()

    grad_two = (cot[...].astype(F32) * slope(pre_two[...].astype(F32))).astype(BF16).astype(F32)
    stage_grad(0, grad_two)
    pl.semaphore_wait(barrier, len(partners))
    g_sent = send_grad(0)
    wide_one = pre_one[...].astype(F32)
    stage_feat(0, (wide_one * jax.nn.sigmoid(wide_one)).reshape(p, HX, C))
    a_sent = send_feat(0)
    stage_feat(1, inputs[...].astype(F32).reshape(p, HX, C))
    build_weights(filt_two)
    gx[:, 0] = jnp.zeros((R, X, 3 * C), BF16)
    gx[:, H + 1] = jnp.zeros((R, X, 3 * C), BF16)
    arrive(relay_grad(0, g_sent))
    build_gx(0)
    data_terms(0)
    a_passed = relay_feat(0, a_sent)
    p_sent = merge_terms(0)
    i_sent = send_feat(1)
    arrive(a_passed)
    build_lhs(0)
    filt_terms(0)
    begin(0, 0, 6)

    delta = part_sum(0, p_sent).reshape(p, H, X, C)
    grad_one = (delta * slope(pre_one[...].astype(F32))).astype(BF16).astype(F32)
    stage_grad(1, grad_one)
    g_sent = send_grad(1)
    begin(0, 6, 18)
    i_passed = relay_feat(1, i_sent)
    go_in(0, 0, 2)
    build_weights(filt_one)
    arrive(i_passed)
    build_lhs(1)
    go_in(0, 2, 6)
    g_passed = relay_grad(1, g_sent)
    go_in(0, 6, 9)
    go_out(0, 0, 3)
    arrive(g_passed)
    build_gx(1)
    go_in(0, 9, 12)
    go_out(0, 3, 7)
    filt_terms(1)
    go_in(0, 12, 16)
    go_out(0, 7, 12)
    data_terms(1)
    go_in(0, 16, 18)
    p_sent = merge_terms(1)
    go_out(0, 12, 18)
    go_in(1, 0, 4)
    out_in[...] = part_sum(1, p_sent).astype(BF16).reshape(p, H, X, C)
    for k in range(4, 18):
        go_in(1, k, k + 1)
        go_out(1, k - 4, k - 3)
    go_out(1, 14, 18)
    for c in pending:
        c.wait_send()
    drain(0)
    drain(1)


def solution(mesh):
    n, m = mesh.shape["rot"], mesh.shape["az"]

    def shards(inputs, pre_one, pre_two, cot, filt_one, filt_two):
        p, H, X, C = inputs.shape
        R, HX, K, nc = n * p, H * X, 9 * p, n // 2
        scale = float(R * H * X * m) ** -0.5
        dma = pltpu.SemaphoreType.DMA
        vmem = pl.BlockSpec(memory_space=pltpu.VMEM)
        sums = jax.ShapeDtypeStruct((K, C, C), BF16)
        got, sum_one, sum_two = pl.pallas_call(
            functools.partial(kernel, n, m, p, H, X, C),
            out_shape=(jax.ShapeDtypeStruct((p, H, X, C), BF16), sums, sums),
            in_specs=[vmem] * 6,
            out_specs=(vmem,) * 3,
            scratch_shapes=[
                pltpu.VMEM((2, p, H, X, C), BF16),
                pltpu.VMEM((2, 2, p * H, C), BF16),
                pltpu.VMEM((2, p, C, HX), BF16),
                pltpu.VMEM((2, n, p, H, X, C), BF16),
                pltpu.VMEM((2, n, 2, p * H, C), BF16),
                pltpu.VMEM((2, n, p, C, HX), BF16),
                pltpu.VMEM((p * C, 9 * C), BF16),
                pltpu.VMEM((R, H + 2, X, 3 * C), BF16),
                pltpu.VMEM((3 * C, (R + p - 1) * HX), BF16),
                pltpu.VMEM((R, HX, p * C), F32),
                pltpu.VMEM((2, n, p, HX, C), BF16),
                pltpu.VMEM((2, nc, p, HX, C), BF16),
                pltpu.VMEM((2, nc, p, HX, C), BF16),
                pltpu.VMEM((2, nc, p, HX, C), BF16),
                pltpu.VMEM((2, K, C, C), BF16),
                pltpu.VMEM((2, 2, K, C, C), BF16),
                pltpu.VMEM((2, K, C, C), BF16),
            ]
            + [dma((2, nc))] * 4
            + [dma((2, 2, nc))] * 2
            + [dma((2, nc))] * 2
            + [dma((2, nc))] * 8
            + [dma((2, K)), dma((2, 2, K)), dma((2, K)), dma((2, K))],
            compiler_params=pltpu.CompilerParams(
                collective_id=0, has_side_effects=True, vmem_limit_bytes=60 * 1024 * 1024
            ),
        )(inputs, pre_one, pre_two, cot, filt_one, filt_two)

        def widen(v):
            return (v.astype(F32) * scale).reshape(p, 3, 3, C, C)

        return got, widen(sum_one), widen(sum_two)

    cells = P("rot", None, "az", None)
    banks = P("rot", None, None, None, None)
    return jax.shard_map(
        shards, mesh=mesh,
        in_specs=(cells,) * 4 + (banks,) * 2,
        out_specs=(cells, banks, banks),
        check_vma=False,
    )
```
